32 devices in a mesh: dp: 16 (over z, y, x), fsdp: 2 (over core).
Axes of the slice: x: 2, y: 2, z: 4, core: 2. Of those that a mesh axis runs over, the one named last changes fastest.
Arguments:
- patches: bfloat16 [1024, 32, 1024], P(('dp', 'fsdp')), may hold values from -6 to 6
- rows: int32 [1024, 32], P(('dp', 'fsdp')), may hold values from 0 to 63
- cols: int32 [1024, 32], P(('dp', 'fsdp')), may hold values from 0 to 63
- keep: int32 [1024, 32], P(('dp', 'fsdp')), may hold values from 0 to 1, as said below
- images: int32 [1024, 32], P(('dp', 'fsdp')), may hold values from 0 to 3, never falling along the last dimension, each value on 1 to 16 neighbouring positions
- destination: int32 [2, 16, 32], P('fsdp'), may hold values from 0 to 15, as said below
- row_table: bfloat16 [64, 1024], replicated, may hold values from -6 to 6
- col_table: bfloat16 [64, 1024], replicated, may hold values from -6 to 6
- w_qkv: bfloat16 [1024, 3072], P('fsdp'), may hold values from -1 to 1
- w_out: bfloat16 [1024, 1024], P('fsdp'), may hold values from -0.1875 to 0.1875
- w_up: bfloat16 [1024, 4096], P('fsdp'), may hold values from -0.1875 to 0.1875
- w_down: bfloat16 [4096, 1024], P('fsdp'), may hold values from -0.09375 to 0.09375
Outputs:
- encoded: bfloat16 [1024, 32, 1024], P(('dp', 'fsdp'))
The draws below stay inside these ranges and needn't reach their ends.
Inputs may be any that keep to these rules, and one draw needn't show every extreme that they name: keep is 0 or 1; the share of kept tokens differs from sequence to sequence. `destination`: for each fsdp index, every dp index is named by exactly 32 entries of the table, and no row names one dp index more than 2 times.
All inputs are finite; a program needn't handle non-finite values.
Results may differ from the reference program's by a relative error of at most 0.0065.
Values may be sent and summed in bfloat16 or wider, within the bound.
A program may use at most 192 MiB of HBM per device.

```python
import math
import jax
import jax.numpy as jnp
import numpy as np
from jax import lax

D = 1024
HEADS = 16
HEAD_DIM = 64
MLP = 4096
SEQ = 32
IMGS = 4
GRID = 64
BLK = 32
PEERS = 16
CAP = 2
BLOCKS = 1024
N_FSDP = 2


def draw_keep(key, part):
    rate_key, coin_key = jax.random.split(jax.random.fold_in(key, 11))
    rates = jax.random.randint(rate_key, (BLOCKS, 1), 30, 96)
    coins = jax.random.randint(coin_key, (BLOCKS, SEQ), 0, 100)
    return (coins < rates).astype(jnp.int32)


def draw_destination(key, part):

    def one_group(group_key):
        first, second, third, fourth = jax.random.split(group_key, 4)
        row_perm = jax.random.permutation(first, PEERS)
        offsets = jnp.tile(jax.random.permutation(second, PEERS), CAP)[:BLK]
        symbol = jax.random.permutation(third, PEERS)
        shuffle = jax.vmap(lambda inner: jax.random.permutation(inner, BLK))(jax.random.split(fourth, PEERS))
        chosen = offsets[shuffle]
        return symbol[(row_perm[:, None] + chosen) % PEERS].astype(jnp.int32)
    return jax.vmap(one_group)(jax.random.split(jax.random.fold_in(key, 23), N_FSDP))


def draw_w_qkv(key, part):
    base_key = jax.random.fold_in(jax.random.fold_in(key, 37), 0)
    base = jnp.clip(jax.random.normal(base_key, (D, 3 * D), jnp.float32), -6.0, 6.0) * D ** (-0.5)
    return jnp.clip(base, -1.0, 1.0).astype(jnp.bfloat16)


def set_ends(entries, own_key, low, high):
    spot = [jax.random.randint(jax.random.fold_in(own_key, axis), (), 0, length) for axis, length in enumerate(entries.shape)]
    main_axis = entries.shape.index(max(entries.shape))
    beside = spot[:main_axis] + [(spot[main_axis] + 1) % entries.shape[main_axis]] + spot[main_axis + 1:]
    return entries.at[tuple(spot)].set(low).at[tuple(beside)].set(high)


def shard_levels(rng, extent, pieces, least, high):
    gain, own = 1.0, jax.random.fold_in(rng, 6)
    for axis_at, blocks in pieces:
        draws = jnp.exp(jax.random.uniform(jax.random.fold_in(own, axis_at), (blocks,), jnp.float32, least / len(pieces), high / len(pieces)))
        gain = gain * jnp.repeat(draws, extent[axis_at] // blocks).reshape([-1 if axis == axis_at else 1 for axis in range(len(extent))])
    return gain


def profile(number_of, total, bound, skew):
    portions = [(1 << 20) // math.isqrt(grade ** skew) + 1 for grade in range(2, number_of + 1)]
    rest, counts = total - bound - (number_of - 1), [1] * (number_of - 1)
    while rest > 0:
        candidates = [i for i in range(number_of - 1) if counts[i] < bound]
        mass, remaining = sum([portions[i] for i in candidates]), rest
        for i in candidates:
            more = min(bound - counts[i], max(1, remaining * portions[i] // mass), rest)
            counts[i] = counts[i] + more
            rest = rest - more
    return np.array([bound] + counts)


def ragged(own_key, number_of, total, bound, lean):
    if number_of == 2:
        one = jax.random.randint(own_key, (), max(1, total - bound), min(bound, total - 1) + 1)
        return jnp.stack([one, total - one])
    sizes = jnp.asarray(profile(number_of, total, bound, lean), jnp.int32)
    couples = (number_of - 1) // 2
    donor, sink = sizes[1:1 + 2 * couples:2], sizes[2:2 + 2 * couples:2]
    room = jnp.minimum(donor - 1, bound - sink)
    moved = jax.random.randint(jax.random.fold_in(own_key, 1), (couples,), 0, 1 << 20) % (room + 1)
    sizes = sizes.at[1:1 + 2 * couples:2].set(donor - moved).at[2:2 + 2 * couples:2].set(sink + moved)
    return sizes[jax.random.permutation(jax.random.fold_in(own_key, 2), number_of)]


def bell_draw(stream_key, dims, scale, most, pieces=(), kind=jnp.bfloat16):
    drawn = jax.random.normal(stream_key, dims, jnp.float32) * scale
    if len(pieces) > 0:
        drawn = shard_levels(stream_key, dims, pieces, -0.22, 0.18) * drawn
    return jnp.clip(drawn, min=-most, max=most).astype(kind)


def setup_inputs(seed: int = 0) -> dict:
    splits = jax.random.split(jax.random.key(seed), 13)
    patches = bell_draw(splits[0], (BLOCKS, SEQ, D), 1.0, 6.0, ((0, 32),))
    rows = set_ends(jax.random.randint(splits[1], (BLOCKS, SEQ), 0, GRID), jax.random.fold_in(splits[1], 1), 0, GRID - 1).astype(jnp.int32)
    cols = set_ends(jax.random.randint(splits[2], (BLOCKS, SEQ), 0, GRID), jax.random.fold_in(splits[2], 1), 0, GRID - 1).astype(jnp.int32)
    keep = draw_keep(jax.random.fold_in(splits[12], 71), 0)
    images = jax.vmap(lambda own: jnp.searchsorted(jnp.cumsum(ragged(own, IMGS, SEQ, SEQ // 2, 0)), jnp.arange(SEQ), side="right"))(jax.random.split(splits[4], BLOCKS)).reshape((BLOCKS, SEQ)).astype(jnp.int32)
    destination = draw_destination(jax.random.fold_in(splits[12], 71), 0)
    row_table = bell_draw(splits[6], (GRID, D), 1.0, 6.0)
    col_table = bell_draw(splits[7], (GRID, D), 1.0, 6.0)
    w_qkv = draw_w_qkv(jax.random.fold_in(splits[12], 71), 0)
    w_out = bell_draw(splits[9], (D, D), D ** -0.5, 0.1875, ((0, 2),))
    w_up = bell_draw(splits[10], (D, MLP), D ** -0.5, 0.1875, ((0, 2),))
    w_down = bell_draw(splits[11], (MLP, D), MLP ** -0.5, 0.09375, ((0, 2),))
    return {"patches": patches, "rows": rows, "cols": cols, "keep": keep, "images": images, "destination": destination, "row_table": row_table, "col_table": col_table, "w_qkv": w_qkv, "w_out": w_out, "w_up": w_up, "w_down": w_down}


EPS = 1e-06

def layer_norm(values):
    center = values - lax.optimization_barrier(jnp.mean(values, axis=-1, keepdims=True))
    spread = lax.optimization_barrier(jnp.mean(center * center, axis=-1, keepdims=True))
    return center * lax.rsqrt(spread + EPS)

def embed(patches, rows, cols, row_table, col_table):
    slots = jnp.arange(GRID, dtype=jnp.int32)
    onehot = jnp.concatenate([(rows[..., None] == slots).astype(jnp.float32), (cols[..., None] == slots).astype(jnp.float32)], axis=-1)
    tables = jnp.concatenate([row_table, col_table], axis=0).astype(jnp.float32)
    places = jnp.einsum('nsg,gd->nsd', onehot, tables)
    return (patches.astype(jnp.float32) + places).astype(jnp.bfloat16)

def encode(embedded, label, w_qkv, w_out, w_up, w_down):
    count, seq, width = embedded.shape
    inputs = embedded.astype(jnp.float32).reshape(count * seq, width)
    normed = layer_norm(inputs).astype(jnp.bfloat16)
    qkv = jnp.dot(normed, w_qkv, preferred_element_type=jnp.float32).astype(jnp.bfloat16)
    parts = qkv.reshape(count, seq, 3, HEADS, HEAD_DIM).astype(jnp.float32)
    scores = jnp.einsum('nqhd,nkhd->nhqk', parts[:, :, 0], parts[:, :, 1]) * HEAD_DIM ** (-0.5)
    allowed = (label[:, :, None] == label[:, None, :]) & (label[:, None, :] > 0)
    allowed = allowed[:, None]
    scores = jnp.where(allowed, scores, -1e+30)
    peak = lax.optimization_barrier(jnp.max(scores, axis=-1, keepdims=True))
    weights = jnp.where(allowed, jnp.exp(scores - peak), 0.0)
    dropped = (label == 0).astype(jnp.float32)[:, None, :, None]
    total = lax.optimization_barrier(jnp.sum(weights, axis=-1, keepdims=True)) + dropped
    probs = (weights / total).astype(jnp.bfloat16).astype(jnp.float32)
    attended = jnp.einsum('nhqk,nkhd->nqhd', probs, parts[:, :, 2]).astype(jnp.bfloat16)
    mid = inputs + jnp.dot(attended.reshape(count * seq, width), w_out, preferred_element_type=jnp.float32)
    second = layer_norm(mid).astype(jnp.bfloat16)
    upper = jnp.dot(second, w_up, preferred_element_type=jnp.float32)
    activated = jax.nn.gelu(upper, approximate=True).astype(jnp.bfloat16)
    result = mid + jnp.dot(activated, w_down, preferred_element_type=jnp.float32)
    live = label.reshape(count * seq, 1) > 0
    return jnp.where(live, result, 0.0).astype(jnp.bfloat16).reshape(count, seq, width)

def placement_order(destination):
    groups, peers, blk = destination.shape
    targets = jnp.arange(peers, dtype=jnp.int32)
    hits = (destination[..., None] == targets).astype(jnp.int32)
    per_source = lax.optimization_barrier(jnp.sum(hits, axis=2)).astype(jnp.int32)
    before = (jnp.cumsum(per_source, axis=1) - per_source).astype(jnp.int32)
    base = jnp.take_along_axis(before, destination, axis=2).astype(jnp.int32)
    within = (jnp.cumsum(hits, axis=2) - hits).astype(jnp.int32)
    within_at = lax.optimization_barrier(jnp.sum(within * hits, axis=3)).astype(jnp.int32)
    rank_at = base + within_at
    group_ids = jnp.arange(groups, dtype=jnp.int32)[:, None, None]
    source_ids = jnp.arange(peers, dtype=jnp.int32)[None, :, None]
    block_ids = jnp.arange(blk, dtype=jnp.int32)[None, None, :]
    source = (source_ids * groups + group_ids) * blk + block_ids
    target = (destination * groups + group_ids) * blk + rank_at
    order = jnp.zeros((groups * peers * blk,), jnp.int32)
    return order.at[target.reshape(-1).astype(jnp.int32)].set(source.reshape(-1).astype(jnp.int32))

def reference(patches, rows, cols, keep, images, destination, row_table, col_table, w_qkv, w_out, w_up, w_down):
    embedded = embed(patches, rows, cols, row_table, col_table)
    label = keep * (images + 1)
    total_blocks = embedded.shape[0]
    grouped = embedded.reshape(total_blocks // BLK, BLK, SEQ, D)
    labels = label.reshape(total_blocks // BLK, BLK, SEQ)

    def one_group(pair):
        return encode(pair[0], pair[1], w_qkv, w_out, w_up, w_down)
    processed = lax.map(one_group, (grouped, labels)).reshape(total_blocks, SEQ, D)
    order = placement_order(destination)
    return jnp.take(processed, order, axis=0)
```

```python
import jax
import jax.numpy as jnp
from jax import lax
from jax.experimental import pallas as pl
from jax.experimental.pallas import tpu as pltpu
from jax.sharding import PartitionSpec as P

HEADS = 16
HEAD_DIM = 64


EPS = 1e-06


def layer_norm(values):
    center = values - jnp.mean(values, axis=-1, keepdims=True)
    spread = jnp.mean(center * center, axis=-1, keepdims=True)
    return center * lax.rsqrt(spread + EPS)


def attend(qkv, label, count, seq):
    parts = qkv.reshape(count, seq, 3, HEADS, HEAD_DIM)
    scores = jnp.einsum(
        "nqhd,nkhd->nhqk", parts[:, :, 0], parts[:, :, 1], preferred_element_type=jnp.float32
    ) * HEAD_DIM ** (-0.5)
    allowed = (label[:, :, None] == label[:, None, :]) & (label[:, None, :] > 0)
    allowed = allowed[:, None]
    scores = jnp.where(allowed, scores, -1e30)
    peak = jnp.max(scores, axis=-1, keepdims=True)
    weights = jnp.where(allowed, jnp.exp(scores - peak), 0.0)
    dropped = (label == 0).astype(jnp.float32)[:, None, :, None]
    total = jnp.sum(weights, axis=-1, keepdims=True) + dropped
    probs = (weights / total).astype(jnp.bfloat16)
    attended = jnp.einsum(
        "nhqk,nkhd->nqhd", probs, parts[:, :, 2], preferred_element_type=jnp.float32
    )
    return attended.astype(jnp.bfloat16).reshape(count * seq, HEADS * HEAD_DIM)


def local(
    patches, rows, cols, keep, images, destination, row_table, col_table, w_qkv, w_out, w_up, w_down
):
    blk, seq, width = patches.shape
    peers = lax.axis_size("dp")
    myself = lax.axis_index("dp")
    capacity = (blk + peers - 1) // peers
    full = (
        lax.all_gather(w_qkv, "fsdp", axis=0, tiled=True),
        lax.all_gather(w_out, "fsdp", axis=0, tiled=True),
        lax.all_gather(w_up, "fsdp", axis=0, tiled=True),
        lax.all_gather(w_down, "fsdp", axis=0, tiled=True),
    )
    grid = row_table.shape[0]
    slots = jnp.arange(grid, dtype=jnp.int32)
    onehot = jnp.concatenate(
        [
            (rows[..., None] == slots).astype(jnp.bfloat16),
            (cols[..., None] == slots).astype(jnp.bfloat16),
        ],
        axis=-1,
    )
    tables = jnp.concatenate([row_table, col_table], axis=0)
    places = jnp.einsum("nsg,gd->nsd", onehot, tables, preferred_element_type=jnp.float32)
    embedded = (patches.astype(jnp.float32) + places).astype(jnp.bfloat16)
    labels = keep * (images + 1)
    table = destination[0]
    mine = lax.dynamic_index_in_dim(table, myself, 0, keepdims=False)
    positions = jnp.arange(blk, dtype=jnp.int32)
    earlier = positions[:, None] > positions[None, :]
    same = mine[:, None] == mine[None, :]
    rank = jnp.sum((same & earlier).astype(jnp.int32), axis=1)
    sending_slot = mine * capacity + rank
    counts = jnp.sum((table == myself).astype(jnp.int32), axis=1)
    arrival = jnp.arange(peers * capacity, dtype=jnp.int32)
    filled = arrival % capacity < jnp.repeat(counts, capacity)
    order = jnp.argsort(jnp.where(filled, arrival, arrival + peers * capacity))[:blk]
    outgoing = (
        jnp.zeros((peers * capacity, seq, width), jnp.bfloat16).at[sending_slot].set(embedded)
    )
    outgoing_labels = (
        jnp.zeros((peers * capacity, seq), jnp.bfloat16)
        .at[sending_slot]
        .set(labels.astype(jnp.bfloat16))
    )
    arrived, arrived_labels = (
        lax.all_to_all(outgoing, "dp", split_axis=0, concat_axis=0, tiled=True),
        lax.all_to_all(outgoing_labels, "dp", split_axis=0, concat_axis=0, tiled=True),
    )
    blocks = jnp.take(arrived, order, axis=0)
    label = jnp.take(arrived_labels, order, axis=0).astype(jnp.float32)
    count = blocks.shape[0]
    inputs = blocks.astype(jnp.float32).reshape(count * seq, width)
    normed = layer_norm(inputs).astype(jnp.bfloat16)
    qkv = jnp.dot(normed, full[0], preferred_element_type=jnp.float32)
    attended = attend(qkv.astype(jnp.bfloat16), label, count, seq)
    projected = jnp.dot(attended, full[1], preferred_element_type=jnp.float32)
    mid = inputs + projected
    second = layer_norm(mid).astype(jnp.bfloat16)
    upper = jnp.dot(second, full[2], preferred_element_type=jnp.float32)
    activated = jax.nn.gelu(upper, approximate=True).astype(jnp.bfloat16)
    lowered = jnp.dot(activated, full[3], preferred_element_type=jnp.float32)
    result = mid + lowered
    live = label.reshape(count * seq, 1) > 0
    return jnp.where(live, result, 0.0).astype(jnp.bfloat16).reshape(count, seq, width)


MESH = pl.DeviceIdType.MESH
ROWS = 128
BF16 = jnp.bfloat16
F32 = jnp.float32


def loop(count, step):
    lax.fori_loop(0, count, lambda i, carry: (step(i), carry)[1], 0)


def layer_kernel(
    perm, onehot, lab, patches, row_table, col_table, w_qkv, w_out, w_up, w_down,
    out,
    pv, tab, wq, wo, wu, wd, x, sb, labs, lsend, normed, qkv, att, mid, alive, res,
    local_sem, w_local, w_send, w_recv, b_send, b_recv, l_send, l_recv, a_send, a_recv,
):
    peers, seq, width = sb.shape
    half = peers * seq
    blocks = half // ROWS
    per = ROWS // seq
    heads = width // (2 * HEAD_DIM)
    mlp = wu.shape[1]
    grid = row_table.shape[0]
    me = lax.axis_index("dp")
    core = lax.axis_index("fsdp")
    other = 1 - core

    barrier = pltpu.get_barrier_semaphore()

    def greet(step):
        peer = lax.rem(me + step + 1, peers)
        pl.semaphore_signal(barrier, inc=1, device_id={"dp": peer}, device_id_type=MESH)

    pl.semaphore_signal(barrier, inc=1, device_id={"fsdp": other}, device_id_type=MESH)
    loop(peers - 1, greet)

    weights = ((w_qkv, wq), (w_out, wo), (w_up, wu), (w_down, wd))

    def own(i):
        src, dst = weights[i]
        return pltpu.make_async_copy(
            src, dst.at[pl.ds(core * src.shape[0], src.shape[0])], w_local.at[i]
        )

    def swap(i):
        src, dst = weights[i]
        return pltpu.make_async_remote_copy(
            src_ref=src,
            dst_ref=dst.at[pl.ds(core * src.shape[0], src.shape[0])],
            send_sem=w_send.at[i],
            recv_sem=w_recv.at[i],
            device_id={"fsdp": other},
            device_id_type=MESH,
        )

    first = (
        pltpu.make_async_copy(patches, pv, local_sem.at[0]),
        pltpu.make_async_copy(row_table, tab.at[pl.ds(0, grid)], local_sem.at[1]),
        pltpu.make_async_copy(col_table, tab.at[pl.ds(grid, grid)], local_sem.at[2]),
    )
    for copy in first:
        copy.start()
    for i in range(4):
        own(i).start()
    for copy in first:
        copy.wait()

    def embed(slot):
        at = perm[slot]
        places = jnp.dot(onehot[at], tab[...], preferred_element_type=F32)
        return (pv[at].astype(F32) + places).astype(BF16)

    def embed_sent(r):
        sb[r] = embed(2 * r + 1)
        lsend[r] = lab[perm[2 * r + 1]]

    loop(peers, embed_sent)

    pl.semaphore_wait(barrier, peers)
    swap(0).start()

    def token_copy(step):
        peer = lax.rem(me + step, peers)
        return pltpu.make_async_remote_copy(
            src_ref=sb.at[peer],
            dst_ref=x.at[1, pl.ds(me * seq, seq)],
            send_sem=b_send.at[step],
            recv_sem=b_recv.at[step],
            device_id={"dp": peer},
            device_id_type=MESH,
        )

    def label_copy(step):
        peer = lax.rem(me + step, peers)
        return pltpu.make_async_remote_copy(
            src_ref=lsend.at[peer],
            dst_ref=labs.at[1, me],
            send_sem=l_send.at[step],
            recv_sem=l_recv.at[step],
            device_id={"dp": peer},
            device_id_type=MESH,
        )

    def send_tokens(i):
        token_copy(i + 1).start()
        label_copy(i + 1).start()

    loop(peers - 1, send_tokens)
    for i in range(1, 4):
        swap(i).start()
    keep_tokens = pltpu.make_async_copy(
        sb.at[me], x.at[1, pl.ds(me * seq, seq)], local_sem.at[3]
    )
    keep_labels = pltpu.make_async_copy(lsend.at[me], labs.at[1, me], local_sem.at[4])
    keep_tokens.start()
    keep_labels.start()

    def embed_kept(r):
        x[0, pl.ds(pl.multiple_of(r * seq, seq), seq)] = embed(2 * r)
        labs[0, r] = lab[perm[2 * r]]

    loop(peers, embed_kept)

    def result_copy(step):
        peer = lax.rem(me + step, peers)
        return pltpu.make_async_remote_copy(
            src_ref=res.at[0, pl.ds(pl.multiple_of(peer * seq, seq), seq)],
            dst_ref=out.at[me, 0],
            send_sem=a_send.at[step],
            recv_sem=a_recv.at[step],
            device_id={"dp": peer},
            device_id_type=MESH,
        )

    keep_result = pltpu.make_async_copy(
        res.at[0, pl.ds(pl.multiple_of(me * seq, seq), seq)], out.at[me, 0], local_sem.at[5]
    )

    lane = lax.broadcasted_iota(jnp.int32, (1, ROWS), 1)
    low = lane < HEAD_DIM
    scale = HEAD_DIM ** (-0.5)
    take_low = jnp.where(low, scale, 0.0).astype(BF16)
    take_high = jnp.where(low, 0.0, scale).astype(BF16)
    ones = jnp.ones((ROWS, ROWS), BF16)

    def ready(h, i):
        @pl.when(h == 0)
        def _():
            own(i).wait()
            swap(i).wait_recv()

    def run(h):
        @pl.when(h == 1)
        def _():
            def arrive(i):
                token_copy(i + 1).wait_recv()
                label_copy(i + 1).wait_recv()

            loop(peers - 1, arrive)
            keep_tokens.wait()
            keep_labels.wait()

        def rows_of(i):
            return pl.ds(pl.multiple_of(i * ROWS, ROWS), ROWS)

        def norm_first(i):
            rows = rows_of(i)
            normed[rows] = layer_norm(x[h, rows].astype(F32)).astype(BF16)

        loop(blocks, norm_first)
        ready(h, 0)
        tile = 512

        def project(n):
            cols = pl.ds(pl.multiple_of(n * tile, tile), tile)
            qkv[:, cols] = jnp.dot(
                normed[...], wq[:, cols], preferred_element_type=F32
            ).astype(BF16)

        loop(3 * width // tile, project)

        def attend_block(i):
            rows = rows_of(i)
            label = jnp.zeros((8, ROWS), jnp.int32)
            for q in range(per):
                label = jnp.where(lane // seq == q, labs[h, i * per + q], label)
            group = jnp.where(label > 0, label + 1024 * (lane // seq), 0).astype(F32)
            row = jnp.broadcast_to(group[0:1], (ROWS, ROWS))
            col = row.T
            alive[rows] = col
            bias = jnp.where((row == col) & (row > 0), 0.0, -1e30)
            bias = jnp.concatenate([bias, bias], axis=0)

            def pair(p):
                def part(third):
                    at = pl.multiple_of(third * width + p * ROWS, ROWS)
                    return qkv[rows, pl.ds(at, ROWS)]

                query = part(0)
                query = jnp.concatenate([query * take_low, query * take_high], axis=0)
                scores = bias + lax.dot_general(
                    query, part(1), (((1,), (1,)), ((), ())), preferred_element_type=F32
                )
                peak = jnp.max(scores, axis=-1, keepdims=True)
                probs = jnp.exp(scores - peak).astype(BF16)
                value = jnp.concatenate([part(2), ones], axis=1)
                mixed = jnp.dot(probs, value, preferred_element_type=F32)
                mixed = jnp.where(low, mixed[:ROWS, :ROWS], mixed[ROWS:, :ROWS]) / jnp.where(
                    low, mixed[:ROWS, ROWS:], mixed[ROWS:, ROWS:]
                )
                att[rows, pl.ds(pl.multiple_of(p * ROWS, ROWS), ROWS)] = mixed.astype(BF16)

            def pairs(p):
                for k in range(4):
                    pair(4 * p + k)

            loop(heads // 4, pairs)

        loop(blocks, attend_block)
        ready(h, 1)

        def project_out(n):
            cols = pl.ds(pl.multiple_of(n * tile, tile), tile)
            mid[:, cols] = x[h, :, cols].astype(F32) + jnp.dot(
                att[...], wo[:, cols], preferred_element_type=F32
            )

        loop(width // tile, project_out)

        def norm_second(i):
            rows = rows_of(i)
            normed[rows] = layer_norm(mid[rows]).astype(BF16)

        loop(blocks, norm_second)
        ready(h, 2)
        ready(h, 3)

        def feed(c):
            cols = pl.ds(pl.multiple_of(c * tile, tile), tile)
            upper = jnp.dot(normed[...], wu[:, cols], preferred_element_type=F32)
            active = jax.nn.gelu(upper, approximate=True).astype(BF16)
            mid[...] += jnp.dot(active, wd[cols], preferred_element_type=F32)

        loop(mlp // tile, feed)

        def finish(i):
            rows = rows_of(i)
            res[h, rows] = jnp.where(alive[rows][:, 0:1] > 0, mid[rows], 0.0).astype(BF16)

        loop(blocks, finish)

        @pl.when(h == 0)
        def _():
            loop(peers - 1, lambda i: result_copy(i + 1).start())
            keep_result.start()

    loop(2, run)

    def store(r):
        return pltpu.make_async_copy(
            res.at[1, pl.ds(pl.multiple_of(r * seq, seq), seq)], out.at[r, 1], b_recv.at[r]
        )

    loop(peers, lambda r: store(r).start())
    keep_result.wait()

    def drain(i):
        token_copy(i + 1).wait_send()
        label_copy(i + 1).wait_send()
        result_copy(i + 1).wait()

    loop(peers - 1, drain)
    for i in range(4):
        swap(i).wait_send()
    loop(peers, lambda r: store(r).wait())


def fused(
    patches, rows, cols, keep, images, destination, row_table, col_table, w_qkv, w_out, w_up, w_down
):
    blk, seq, width = patches.shape
    peers = lax.axis_size("dp")
    grid = row_table.shape[0]
    mlp = w_up.shape[1]
    slots = jnp.arange(grid, dtype=jnp.int32)
    onehot = jnp.concatenate(
        [(rows[..., None] == slots).astype(BF16), (cols[..., None] == slots).astype(BF16)],
        axis=-1,
    )
    labels = jnp.tile(keep * (images + 1), (1, ROWS // seq))
    labels = jnp.broadcast_to(labels[:, None], (blk, 8, ROWS))
    mine = lax.dynamic_index_in_dim(destination[0], lax.axis_index("dp"), 0, keepdims=False)
    positions = jnp.arange(blk, dtype=jnp.int32)
    ahead = (mine[:, None] > mine[None, :]) | (
        (mine[:, None] == mine[None, :]) & (positions[:, None] > positions[None, :])
    )
    place = jnp.sum(ahead.astype(jnp.int32), axis=1)
    perm = jnp.sum(jnp.where(place[None, :] == positions[:, None], positions[None, :], 0), axis=1)
    half = peers * seq
    anywhere = pl.BlockSpec(memory_space=pl.ANY)
    vmem = pl.BlockSpec(memory_space=pltpu.VMEM)
    dma = pltpu.SemaphoreType.DMA
    out = pl.pallas_call(
        layer_kernel,
        out_shape=jax.ShapeDtypeStruct((peers, blk // peers, seq, width), BF16),
        in_specs=[pl.BlockSpec(memory_space=pltpu.SMEM), vmem, vmem] + [anywhere] * 7,
        out_specs=anywhere,
        scratch_shapes=[
            pltpu.VMEM((blk, seq, width), BF16),
            pltpu.VMEM((2 * grid, width), BF16),
            pltpu.VMEM((width, 3 * width), BF16),
            pltpu.VMEM((width, width), BF16),
            pltpu.VMEM((width, mlp), BF16),
            pltpu.VMEM((mlp, width), BF16),
            pltpu.VMEM((2, half, width), BF16),
            pltpu.VMEM((peers, seq, width), BF16),
            pltpu.VMEM((2, peers, 8, ROWS), jnp.int32),
            pltpu.VMEM((peers, 8, ROWS), jnp.int32),
            pltpu.VMEM((half, width), BF16),
            pltpu.VMEM((half, 3 * width), BF16),
            pltpu.VMEM((half, width), BF16),
            pltpu.VMEM((half, width), F32),
            pltpu.VMEM((half, ROWS), F32),
            pltpu.VMEM((2, half, width), BF16),
            dma((6,)),
            dma((4,)),
            dma((4,)),
            dma((4,)),
            dma((peers,)),
            dma((peers,)),
            dma((peers,)),
            dma((peers,)),
            dma((peers,)),
            dma((peers,)),
        ],
        compiler_params=pltpu.CompilerParams(
            collective_id=0, has_side_effects=True, vmem_limit_bytes=60 * 1024 * 1024
        ),
    )(perm, onehot, labels, patches, row_table, col_table, w_qkv, w_out, w_up, w_down)
    return out.reshape(blk, seq, width)


def choose(*args):
    blk, seq, width = args[0].shape
    peers = lax.axis_size("dp")
    even = blk == 2 * peers and lax.axis_size("fsdp") == 2
    fits = ROWS % seq == 0 and (peers * seq) % ROWS == 0 and width % 1024 == 0
    return (fused if even and fits else local)(*args)


def solution(mesh):
    in_specs = (
        P(("dp", "fsdp"), None, None),
        P(("dp", "fsdp"), None),
        P(("dp", "fsdp"), None),
        P(("dp", "fsdp"), None),
        P(("dp", "fsdp"), None),
        P("fsdp", None, None),
        P(),
        P(),
        P("fsdp", None),
        P("fsdp", None),
        P("fsdp", None),
        P("fsdp", None),
    )
    out_specs = P(("dp", "fsdp"), None, None)
    return jax.shard_map(choose, mesh=mesh, in_specs=in_specs, out_specs=out_specs, check_vma=False)
```

```python
import jax
import jax.numpy as jnp
from jax import lax
from jax.experimental import pallas as pl
from jax.experimental.pallas import tpu as pltpu
from jax.sharding import PartitionSpec as P

HEADS = 16
HEAD_DIM = 64


EPS = 1e-06


def layer_norm(values):
    center = values - jnp.mean(values, axis=-1, keepdims=True)
    spread = jnp.mean(center * center, axis=-1, keepdims=True)
    return center * lax.rsqrt(spread + EPS)


def attend(qkv, label, count, seq):
    parts = qkv.reshape(count, seq, 3, HEADS, HEAD_DIM)
    scores = jnp.einsum(
        "nqhd,nkhd->nhqk", parts[:, :, 0], parts[:, :, 1], preferred_element_type=jnp.float32
    ) * HEAD_DIM ** (-0.5)
    allowed = (label[:, :, None] == label[:, None, :]) & (label[:, None, :] > 0)
    allowed = allowed[:, None]
    scores = jnp.where(allowed, scores, -1e30)
    peak = jnp.max(scores, axis=-1, keepdims=True)
    weights = jnp.where(allowed, jnp.exp(scores - peak), 0.0)
    dropped = (label == 0).astype(jnp.float32)[:, None, :, None]
    total = jnp.sum(weights, axis=-1, keepdims=True) + dropped
    probs = (weights / total).astype(jnp.bfloat16)
    attended = jnp.einsum(
        "nhqk,nkhd->nqhd", probs, parts[:, :, 2], preferred_element_type=jnp.float32
    )
    return attended.astype(jnp.bfloat16).reshape(count * seq, HEADS * HEAD_DIM)


def local(
    patches, rows, cols, keep, images, destination, row_table, col_table, w_qkv, w_out, w_up, w_down
):
    blk, seq, width = patches.shape
    peers = lax.axis_size("dp")
    myself = lax.axis_index("dp")
    capacity = (blk + peers - 1) // peers
    full = (
        lax.all_gather(w_qkv, "fsdp", axis=0, tiled=True),
        lax.all_gather(w_out, "fsdp", axis=0, tiled=True),
        lax.all_gather(w_up, "fsdp", axis=0, tiled=True),
        lax.all_gather(w_down, "fsdp", axis=0, tiled=True),
    )
    grid = row_table.shape[0]
    slots = jnp.arange(grid, dtype=jnp.int32)
    onehot = jnp.concatenate(
        [
            (rows[..., None] == slots).astype(jnp.bfloat16),
            (cols[..., None] == slots).astype(jnp.bfloat16),
        ],
        axis=-1,
    )
    tables = jnp.concatenate([row_table, col_table], axis=0)
    places = jnp.einsum("nsg,gd->nsd", onehot, tables, preferred_element_type=jnp.float32)
    embedded = (patches.astype(jnp.float32) + places).astype(jnp.bfloat16)
    labels = keep * (images + 1)
    table = destination[0]
    mine = lax.dynamic_index_in_dim(table, myself, 0, keepdims=False)
    positions = jnp.arange(blk, dtype=jnp.int32)
    earlier = positions[:, None] > positions[None, :]
    same = mine[:, None] == mine[None, :]
    rank = jnp.sum((same & earlier).astype(jnp.int32), axis=1)
    sending_slot = mine * capacity + rank
    counts = jnp.sum((table == myself).astype(jnp.int32), axis=1)
    arrival = jnp.arange(peers * capacity, dtype=jnp.int32)
    filled = arrival % capacity < jnp.repeat(counts, capacity)
    order = jnp.argsort(jnp.where(filled, arrival, arrival + peers * capacity))[:blk]
    outgoing = (
        jnp.zeros((peers * capacity, seq, width), jnp.bfloat16).at[sending_slot].set(embedded)
    )
    outgoing_labels = (
        jnp.zeros((peers * capacity, seq), jnp.bfloat16)
        .at[sending_slot]
        .set(labels.astype(jnp.bfloat16))
    )
    arrived, arrived_labels = (
        lax.all_to_all(outgoing, "dp", split_axis=0, concat_axis=0, tiled=True),
        lax.all_to_all(outgoing_labels, "dp", split_axis=0, concat_axis=0, tiled=True),
    )
    blocks = jnp.take(arrived, order, axis=0)
    label = jnp.take(arrived_labels, order, axis=0).astype(jnp.float32)
    count = blocks.shape[0]
    inputs = blocks.astype(jnp.float32).reshape(count * seq, width)
    normed = layer_norm(inputs).astype(jnp.bfloat16)
    qkv = jnp.dot(normed, full[0], preferred_element_type=jnp.float32)
    attended = attend(qkv.astype(jnp.bfloat16), label, count, seq)
    projected = jnp.dot(attended, full[1], preferred_element_type=jnp.float32)
    mid = inputs + projected
    second = layer_norm(mid).astype(jnp.bfloat16)
    upper = jnp.dot(second, full[2], preferred_element_type=jnp.float32)
    activated = jax.nn.gelu(upper, approximate=True).astype(jnp.bfloat16)
    lowered = jnp.dot(activated, full[3], preferred_element_type=jnp.float32)
    result = mid + lowered
    live = label.reshape(count * seq, 1) > 0
    return jnp.where(live, result, 0.0).astype(jnp.bfloat16).reshape(count, seq, width)


MESH = pl.DeviceIdType.MESH
ROWS = 128
BF16 = jnp.bfloat16
F32 = jnp.float32


def loop(count, step):
    lax.fori_loop(0, count, lambda i, carry: (step(i), carry)[1], 0)


def layer_kernel(
    perm, rows_in, cols_in, keep_in, images_in, patches, row_table, col_table, w_qkv, w_out, w_up, w_down,
    out,
    rows, cols, keep, images, pv, tab, wq, wo, wu, wd, x, sb, labs, lsend, normed, qkv, att, mid, alive, res,
    local_sem, w_local, w_send, w_recv, b_send, b_recv, l_send, l_recv, a_send, a_recv,
):
    peers, seq, width = sb.shape
    half = peers * seq
    blocks = half // ROWS
    per = ROWS // seq
    heads = width // (2 * HEAD_DIM)
    mlp = wu.shape[1]
    grid = row_table.shape[0]
    me = lax.axis_index("dp")
    core = lax.axis_index("fsdp")
    other = 1 - core

    barrier = pltpu.get_barrier_semaphore()

    def greet(step):
        peer = lax.rem(me + step + 1, peers)
        pl.semaphore_signal(barrier, inc=1, device_id={"dp": peer}, device_id_type=MESH)

    pl.semaphore_signal(barrier, inc=1, device_id={"fsdp": other}, device_id_type=MESH)
    loop(peers - 1, greet)

    weights = ((w_qkv, wq), (w_out, wo), (w_up, wu), (w_down, wd))

    def own(i):
        src, dst = weights[i]
        return pltpu.make_async_copy(
            src, dst.at[pl.ds(core * src.shape[0], src.shape[0])], w_local.at[i]
        )

    tile = 512
    pieces = 3 * width // tile

    def swap(i):
        src, dst = weights[i]
        return pltpu.make_async_remote_copy(
            src_ref=src,
            dst_ref=dst.at[pl.ds(core * src.shape[0], src.shape[0])],
            send_sem=w_send.at[pieces + i],
            recv_sem=w_recv.at[pieces + i],
            device_id={"fsdp": other},
            device_id_type=MESH,
        )

    def swap_piece(n):
        cols = pl.ds(pl.multiple_of(n * tile, tile), tile)
        return pltpu.make_async_remote_copy(
            src_ref=w_qkv.at[:, cols],
            dst_ref=wq.at[pl.ds(core * w_qkv.shape[0], w_qkv.shape[0]), cols],
            send_sem=w_send.at[n],
            recv_sem=w_recv.at[n],
            device_id={"fsdp": other},
            device_id_type=MESH,
        )

    first = (
        pltpu.make_async_copy(patches, pv, local_sem.at[0]),
        pltpu.make_async_copy(row_table, tab.at[pl.ds(0, grid)], local_sem.at[1]),
        pltpu.make_async_copy(col_table, tab.at[pl.ds(grid, grid)], local_sem.at[2]),
        pltpu.make_async_copy(rows_in, rows, local_sem.at[6]),
        pltpu.make_async_copy(cols_in, cols, local_sem.at[7]),
        pltpu.make_async_copy(keep_in, keep, local_sem.at[8]),
        pltpu.make_async_copy(images_in, images, local_sem.at[9]),
    )
    for copy in first:
        copy.start()
    for i in range(4):
        own(i).start()
    for copy in first:
        copy.wait()

    def embed(i, which, target, tags):
        at = [perm[2 * (i * per + q) + which] for q in range(per)]
        row = jnp.concatenate([rows[pl.ds(a, 1)] for a in at], axis=1)
        col = jnp.concatenate([cols[pl.ds(a, 1)] for a in at], axis=1)
        spot = lax.broadcasted_iota(jnp.int32, (ROWS, ROWS), 0)
        hot = jnp.where(spot < grid, row, col + grid) == spot
        hot = jnp.where(hot, 1.0, 0.0).T.astype(BF16)
        places = jnp.dot(hot, tab[...], preferred_element_type=F32)
        for q in range(per):
            place = places[q * seq:(q + 1) * seq]
            target(i * per + q, (pv[at[q]].astype(F32) + place).astype(BF16))
            tag = keep[pl.ds(at[q], 1)] * (images[pl.ds(at[q], 1)] + 1)
            tags[i * per + q] = jnp.broadcast_to(jnp.concatenate([tag] * per, axis=1), (8, ROWS))

    def set_sent(r, value):
        sb[r] = value

    def set_kept(r, value):
        x[0, pl.ds(pl.multiple_of(r * seq, seq), seq)] = value

    loop(blocks, lambda i: embed(i, 1, set_sent, lsend))

    pl.semaphore_wait(barrier, peers)
    loop(pieces, lambda n: swap_piece(n).start())

    def token_copy(step):
        peer = lax.rem(me + step, peers)
        return pltpu.make_async_remote_copy(
            src_ref=sb.at[peer],
            dst_ref=x.at[1, pl.ds(me * seq, seq)],
            send_sem=b_send.at[step],
            recv_sem=b_recv.at[step],
            device_id={"dp": peer},
            device_id_type=MESH,
        )

    def label_copy(step):
        peer = lax.rem(me + step, peers)
        return pltpu.make_async_remote_copy(
            src_ref=lsend.at[peer],
            dst_ref=labs.at[1, me],
            send_sem=l_send.at[step],
            recv_sem=l_recv.at[step],
            device_id={"dp": peer},
            device_id_type=MESH,
        )

    def send_tokens(i):
        token_copy(i + 1).start()
        label_copy(i + 1).start()

    loop(peers - 1, send_tokens)
    for i in range(1, 4):
        swap(i).start()
    keep_tokens = pltpu.make_async_copy(
        sb.at[me], x.at[1, pl.ds(me * seq, seq)], local_sem.at[3]
    )
    keep_labels = pltpu.make_async_copy(lsend.at[me], labs.at[1, me], local_sem.at[4])
    keep_tokens.start()
    keep_labels.start()

    loop(blocks, lambda i: embed(i, 0, set_kept, labs.at[0]))

    def result_copy(step):
        peer = lax.rem(me + step, peers)
        return pltpu.make_async_remote_copy(
            src_ref=res.at[0, pl.ds(pl.multiple_of(peer * seq, seq), seq)],
            dst_ref=out.at[me, 0],
            send_sem=a_send.at[step],
            recv_sem=a_recv.at[step],
            device_id={"dp": peer},
            device_id_type=MESH,
        )

    keep_result = pltpu.make_async_copy(
        res.at[0, pl.ds(pl.multiple_of(me * seq, seq), seq)], out.at[me, 0], local_sem.at[5]
    )

    lane = lax.broadcasted_iota(jnp.int32, (1, ROWS), 1)
    low = lane < HEAD_DIM
    scale = HEAD_DIM ** (-0.5)
    take_low = jnp.where(low, scale, 0.0).astype(BF16)
    take_high = jnp.where(low, 0.0, scale).astype(BF16)
    ones = jnp.ones((ROWS, ROWS), BF16)

    def ready(h, i):
        @pl.when(h == 0)
        def _():
            own(i).wait()
            swap(i).wait_recv()

    def ready_own(h, i):
        @pl.when(h == 0)
        def _():
            own(i).wait()

    def run(h):
        @pl.when(h == 1)
        def _():
            def arrive(i):
                token_copy(i + 1).wait_recv()
                label_copy(i + 1).wait_recv()

            loop(peers - 1, arrive)
            keep_tokens.wait()
            keep_labels.wait()

        def rows_of(i):
            return pl.ds(pl.multiple_of(i * ROWS, ROWS), ROWS)

        def norm_first(i):
            rows = rows_of(i)
            normed[rows] = layer_norm(x[h, rows].astype(F32)).astype(BF16)

        loop(blocks, norm_first)
        ready_own(h, 0)

        def project(n):
            @pl.when(h == 0)
            def _():
                swap_piece(n).wait_recv()

            cols = pl.ds(pl.multiple_of(n * tile, tile), tile)
            qkv[:, cols] = jnp.dot(
                normed[...], wq[:, cols], preferred_element_type=F32
            ).astype(BF16)

        loop(pieces, project)

        def attend_block(i):
            rows = rows_of(i)
            label = jnp.zeros((8, ROWS), jnp.int32)
            for q in range(per):
                label = jnp.where(lane // seq == q, labs[h, i * per + q], label)
            group = jnp.where(label > 0, label + 1024 * (lane // seq), 0).astype(F32)
            row = jnp.broadcast_to(group[0:1], (ROWS, ROWS))
            col = row.T
            alive[rows] = col
            bias = jnp.where((row == col) & (row > 0), 0.0, -1e30)
            bias = jnp.concatenate([bias, bias], axis=0)

            def pair(p):
                def part(third):
                    at = pl.multiple_of(third * width + p * ROWS, ROWS)
                    return qkv[rows, pl.ds(at, ROWS)]

                query = part(0)
                query = jnp.concatenate([query * take_low, query * take_high], axis=0)
                scores = bias + lax.dot_general(
                    query, part(1), (((1,), (1,)), ((), ())), preferred_element_type=F32
                )
                peak = jnp.max(scores, axis=-1, keepdims=True)
                probs = jnp.exp(scores - peak).astype(BF16)
                value = jnp.concatenate([part(2), ones], axis=1)
                mixed = jnp.dot(probs, value, preferred_element_type=F32)
                mixed = jnp.where(low, mixed[:ROWS, :ROWS], mixed[ROWS:, :ROWS]) / jnp.where(
                    low, mixed[:ROWS, ROWS:], mixed[ROWS:, ROWS:]
                )
                att[rows, pl.ds(pl.multiple_of(p * ROWS, ROWS), ROWS)] = mixed.astype(BF16)

            def pairs(p):
                for k in range(8):
                    pair(8 * p + k)

            loop(heads // 8, pairs)

        loop(blocks, attend_block)
        ready(h, 1)

        def project_out(n):
            cols = pl.ds(pl.multiple_of(n * tile, tile), tile)
            mid[:, cols] = x[h, :, cols].astype(F32) + jnp.dot(
                att[...], wo[:, cols], preferred_element_type=F32
            )

        loop(width // tile, project_out)

        def norm_second(i):
            rows = rows_of(i)
            normed[rows] = layer_norm(mid[rows]).astype(BF16)

        loop(blocks, norm_second)
        ready(h, 2)
        ready_own(h, 3)
        wide = 1024
        steps = mlp // wide

        def feed(step):
            @pl.when((h == 0) & (step == steps // 2))
            def _():
                swap(3).wait_recv()

            c = lax.rem(step + core * (steps // 2), steps)
            cols = pl.ds(pl.multiple_of(c * wide, wide), wide)
            upper = jnp.dot(normed[...], wu[:, cols], preferred_element_type=F32)
            active = jax.nn.gelu(upper, approximate=True).astype(BF16)
            mid[...] += jnp.dot(active, wd[cols], preferred_element_type=F32)

        loop(steps, feed)

        def finish(i):
            rows = rows_of(i)
            res[h, rows] = jnp.where(alive[rows][:, 0:1] > 0, mid[rows], 0.0).astype(BF16)

        loop(blocks, finish)

        @pl.when(h == 0)
        def _():
            loop(peers - 1, lambda i: result_copy(i + 1).start())
            keep_result.start()

    loop(2, run)

    def store(r):
        return pltpu.make_async_copy(
            res.at[1, pl.ds(pl.multiple_of(r * seq, seq), seq)], out.at[r, 1], b_recv.at[r]
        )

    loop(peers, lambda r: store(r).start())
    keep_result.wait()

    def drain(i):
        token_copy(i + 1).wait_send()
        label_copy(i + 1).wait_send()
        result_copy(i + 1).wait()

    loop(peers - 1, drain)
    loop(pieces, lambda n: swap_piece(n).wait_send())
    for i in range(1, 4):
        swap(i).wait_send()
    loop(peers, lambda r: store(r).wait())


def fused(
    patches, rows, cols, keep, images, destination, row_table, col_table, w_qkv, w_out, w_up, w_down
):
    blk, seq, width = patches.shape
    peers = lax.axis_size("dp")
    grid = row_table.shape[0]
    mlp = w_up.shape[1]
    mine = lax.dynamic_index_in_dim(destination[0], lax.axis_index("dp"), 0, keepdims=False)
    positions = jnp.arange(blk, dtype=jnp.int32)
    ahead = (mine[:, None] > mine[None, :]) | (
        (mine[:, None] == mine[None, :]) & (positions[:, None] > positions[None, :])
    )
    place = jnp.sum(ahead.astype(jnp.int32), axis=1)
    perm = jnp.sum(jnp.where(place[None, :] == positions[:, None], positions[None, :], 0), axis=1)
    half = peers * seq
    anywhere = pl.BlockSpec(memory_space=pl.ANY)
    hbm = pl.BlockSpec(memory_space=pltpu.HBM)
    dma = pltpu.SemaphoreType.DMA
    out = pl.pallas_call(
        layer_kernel,
        out_shape=jax.ShapeDtypeStruct((peers, blk // peers, seq, width), BF16),
        in_specs=[pl.BlockSpec(memory_space=pltpu.SMEM)] + [hbm] * 11,
        out_specs=anywhere,
        scratch_shapes=[
            pltpu.VMEM((blk, seq), jnp.int32),
            pltpu.VMEM((blk, seq), jnp.int32),
            pltpu.VMEM((blk, seq), jnp.int32),
            pltpu.VMEM((blk, seq), jnp.int32),
            pltpu.VMEM((blk, seq, width), BF16),
            pltpu.VMEM((2 * grid, width), BF16),
            pltpu.VMEM((width, 3 * width), BF16),
            pltpu.VMEM((width, width), BF16),
            pltpu.VMEM((width, mlp), BF16),
            pltpu.VMEM((mlp, width), BF16),
            pltpu.VMEM((2, half, width), BF16),
            pltpu.VMEM((peers, seq, width), BF16),
            pltpu.VMEM((2, peers, 8, ROWS), jnp.int32),
            pltpu.VMEM((peers, 8, ROWS), jnp.int32),
            pltpu.VMEM((half, width), BF16),
            pltpu.VMEM((half, 3 * width), BF16),
            pltpu.VMEM((half, width), BF16),
            pltpu.VMEM((half, width), F32),
            pltpu.VMEM((half, ROWS), F32),
            pltpu.VMEM((2, half, width), BF16),
            dma((10,)),
            dma((4,)),
            dma((3 * width // 512 + 4,)),
            dma((3 * width // 512 + 4,)),
            dma((peers,)),
            dma((peers,)),
            dma((peers,)),
            dma((peers,)),
            dma((peers,)),
            dma((peers,)),
        ],
        compiler_params=pltpu.CompilerParams(
            collective_id=0, has_side_effects=True, vmem_limit_bytes=60 * 1024 * 1024
        ),
    )(perm, rows, cols, keep, images, patches, row_table, col_table, w_qkv, w_out, w_up, w_down)
    return out.reshape(blk, seq, width)


def choose(*args):
    blk, seq, width = args[0].shape
    peers = lax.axis_size("dp")
    even = blk == 2 * peers and lax.axis_size("fsdp") == 2
    fits = 2 * args[6].shape[0] == ROWS and ROWS % seq == 0 and (peers * seq) % ROWS == 0 and width % 1024 == 0
    return (fused if even and fits else local)(*args)


def solution(mesh):
    in_specs = (
        P(("dp", "fsdp"), None, None),
        P(("dp", "fsdp"), None),
        P(("dp", "fsdp"), None),
        P(("dp", "fsdp"), None),
        P(("dp", "fsdp"), None),
        P("fsdp", None, None),
        P(),
        P(),
        P("fsdp", None),
        P("fsdp", None),
        P("fsdp", None),
        P("fsdp", None),
    )
    out_specs = P(("dp", "fsdp"), None, None)
    return jax.shard_map(choose, mesh=mesh, in_specs=in_specs, out_specs=out_specs, check_vma=False)
```
